512 devices in a mesh: req: 64 (over y, x, core), tp: 8 (over z).
Axes of the slice: x: 4, y: 8, z: 8, core: 2. Of those that a mesh axis runs over, the one named last changes fastest.
Arguments:
- tokens: bfloat16 [13312, 2048], P('req', 'tp'), may hold values from -6 to 6
- ln_gain: bfloat16 [2048], P('tp'), may hold values from 0.099609375 to 1.8984375
- ln_bias: bfloat16 [2048], P('tp'), may hold values from -3 to 3
- w_qkv: bfloat16 [2048, 3, 1024], P(None, None, 'tp'), may hold values from -3 to 3
- qkv_bias: bfloat16 [3, 1024], P(None, 'tp'), may hold values from -3 to 3
- w_dense: bfloat16 [1024, 2048], P('tp'), may hold values from -0.1875 to 0.1875
- dense_bias: bfloat16 [2048], P('tp'), may hold values from -3 to 3
- prefix_kv: bfloat16 [1024, 32, 2, 1024], P('req', None, None, 'tp'), may hold values from -6 to 6
- lengths: int32 [64, 16], replicated, may hold values from 1 to 16, 208 in all within a row
- owner_slot: int32 [1024], replicated, may hold values from 0 to 1023, as said below
Outputs:
- attended: bfloat16 [13312, 2048], P('req', 'tp')
- new_cache: bfloat16 [1024, 16, 2, 1024], P('req', None, None, 'tp')
The draws below stay inside these ranges and needn't reach their ends.
Inputs may be any that keep to these rules, and one draw needn't show every extreme that they name: owner_slot names every slot once; owner_slot[g] % 16 == g % 16; two requests of one req index name slots on the same req index only if their j differ by a multiple of 64, so one req index sends exactly 1 request to each req index that it sends to. `lengths`: each row sums to 208 and reaches 16.
All inputs are finite; a program needn't handle non-finite values.
Results may differ from the reference program's by a relative error of at most 0.014.
Values may be sent and summed in bfloat16 or wider, within the bound.
No kernel may reach another device: no remote copies, remote signals or barrier semaphores. Data moves between devices by JAX's collectives and lax.ppermute only.
A program may use at most 64 MiB of HBM per device.

```python
import math
import jax
import jax.numpy as jnp
import numpy as np
from jax import lax

D = 2048
HD = 128
HEADS = 8
LMAX = 16
PRE = 32
R_DEV = 16
TOK_DEV = 208
SHARDS = 64
REQS = 1024
TOKENS = 13312
N_TP = 8


def owner_law(key):
    outer_perm = jax.random.permutation(jax.random.fold_in(key, 101), SHARDS).astype(jnp.int32)
    inner_perm = jax.random.permutation(jax.random.fold_in(key, 202), SHARDS).astype(jnp.int32)
    shard_ids = jnp.arange(SHARDS, dtype=jnp.int32)[:, None]
    slot_ids = jnp.arange(R_DEV, dtype=jnp.int32)[None, :]
    owners = outer_perm[(inner_perm[shard_ids] + slot_ids) % SHARDS]
    return (owners * R_DEV + slot_ids).reshape(-1).astype(jnp.int32)


def draw_owner_slot(key, part):
    return owner_law(key)


def draw_w_qkv(key, part):
    head_cols = HEADS * HD
    normal_part = jnp.clip(jax.random.normal(jax.random.fold_in(key, 7), (D, 3, head_cols), jnp.float32), -4.0, 4.0) * (1.0 / math.sqrt(D))
    return normal_part.astype(jnp.bfloat16)


def levels(stream_key, extent, shards, least, top_value):
    def one(position, shards_of):
        heights = jax.random.uniform(jax.random.fold_in(jax.random.fold_in(stream_key, 6), position), (shards_of,), jnp.float32, least / len(shards), top_value / len(shards))
        return jnp.repeat(jnp.exp(heights), extent[position] // shards_of).reshape((-1,) + (1,) * (len(extent) - position - 1))

    level = one(*shards[0])
    for cut in shards[1:]:
        level = level * one(*cut)
    return level


def length_profile(number_of, total, reach, slope):
    loads = [(1 << 20) // math.isqrt(grade ** slope) + 1 for grade in range(2, number_of + 1)]
    surplus, counts = total - reach - (number_of - 1), [1] * (number_of - 1)
    while surplus > 0:
        free = [i for i in range(number_of - 1) if counts[i] < reach]
        mass, left = sum([loads[i] for i in free]), surplus
        for i in free:
            addition = min(reach - counts[i], max(1, left * loads[i] // mass), surplus)
            counts[i] = counts[i] + addition
            surplus = surplus - addition
    return np.array([reach] + counts)


def uneven_parts(rng, amount, total, most, skew):
    if amount == 2:
        one = jax.random.randint(rng, (), max(1, total - most), min(most, total - 1) + 1)
        return jnp.stack([one, total - one])
    sizes = jnp.asarray(length_profile(amount, total, most, skew), jnp.int32)
    couples = (amount - 1) // 2
    giver, receiver = sizes[1:1 + 2 * couples:2], sizes[2:2 + 2 * couples:2]
    slack = jnp.minimum(giver - 1, most - receiver)
    moved = jax.random.randint(jax.random.fold_in(rng, 1), (couples,), 0, 1 << 20) % (slack + 1)
    sizes = sizes.at[1:1 + 2 * couples:2].set(giver - moved).at[2:2 + 2 * couples:2].set(receiver + moved)
    return sizes[jax.random.permutation(jax.random.fold_in(rng, 2), amount)]


def gaussian(own_key, shape, spread, most, cuts=(), kind=jnp.bfloat16):
    drawn = spread * jax.random.normal(own_key, shape, jnp.float32)
    if cuts:
        drawn = drawn * levels(own_key, shape, cuts, -0.22, 0.18)
    return jnp.clip(drawn, -most, most).astype(kind)


def setup_inputs(seed: int = 0) -> dict:
    splits = jax.random.split(jax.random.key(seed), 11)
    tokens = gaussian(splits[0], (TOKENS, D), 1.0, 6.0, ((0, 64), (1, 8)))
    ln_gain = jnp.clip(1.0 + 0.18 * jax.random.normal(splits[1], (D,), jnp.float32), 0.099609375, 1.8984375).astype(jnp.bfloat16)
    ln_bias = gaussian(splits[2], (D,), 0.5, 3.0, ((0, 8),))
    w_qkv = draw_w_qkv(jax.random.fold_in(splits[10], 71), 0)
    qkv_bias = gaussian(splits[4], (3, HEADS * HD), 0.5, 3.0, ((1, 8),))
    w_dense = gaussian(splits[5], (HEADS * HD, D), (HEADS * HD) ** -0.5, 0.1875, ((0, 8),))
    dense_bias = gaussian(splits[6], (D,), 0.5, 3.0, ((0, 8),))
    prefix_kv = gaussian(splits[7], (REQS, PRE, 2, HEADS * HD), 1.0, 6.0, ((0, 64), (3, 8)))
    lengths = jax.vmap(lambda own: uneven_parts(own, R_DEV, TOK_DEV, LMAX, 2))(jax.random.split(splits[8], SHARDS)).reshape((SHARDS, R_DEV)).astype(jnp.int32)
    owner_slot = draw_owner_slot(jax.random.fold_in(splits[10], 71), 0)
    return dict(tokens=tokens, ln_gain=ln_gain, ln_bias=ln_bias, w_qkv=w_qkv, qkv_bias=qkv_bias, w_dense=w_dense, dense_bias=dense_bias, prefix_kv=prefix_kv, lengths=lengths, owner_slot=owner_slot)


def layer_norm(row_block, gain_vec, shift_vec):
    values = row_block.astype(jnp.float32)
    width = values.shape[-1]
    mean_val = lax.optimization_barrier(jnp.sum(values, axis=-1, keepdims=True)) / width
    second = lax.optimization_barrier(jnp.sum(values * values, axis=-1, keepdims=True)) / width
    scale_inv = lax.rsqrt(second - mean_val * mean_val + 1e-05)
    return ((values - mean_val) * scale_inv * gain_vec.astype(jnp.float32) + shift_vec.astype(jnp.float32)).astype(jnp.bfloat16)

def attend(queries, all_keys, all_values, slopes, prefix_len):
    span = all_keys.shape[1]
    steps_new = queries.shape[1]
    scores = jnp.einsum('rqhd,rkhd->rhqk', queries.astype(jnp.float32), all_keys.astype(jnp.float32)) / math.sqrt(HD)
    distance = (prefix_len + jnp.arange(steps_new, dtype=jnp.int32))[:, None] - jnp.arange(span, dtype=jnp.int32)[None, :]
    scores = scores - slopes[None, :, None, None] * distance.astype(jnp.float32)[None, None]
    scores = jnp.where((distance >= 0)[None, None], scores, -jnp.inf)
    row_max = lax.optimization_barrier(jnp.max(scores, axis=-1, keepdims=True))
    raised = jnp.exp(scores - row_max)
    weights = (raised / lax.optimization_barrier(jnp.sum(raised, axis=-1, keepdims=True))).astype(jnp.bfloat16)
    return jnp.einsum('rhqk,rkhd->rqhd', weights.astype(jnp.float32), all_values.astype(jnp.float32)).astype(jnp.bfloat16)

def reference(tokens, ln_gain, ln_bias, w_qkv, qkv_bias, w_dense, dense_bias, prefix_kv, lengths, owner_slot):
    head_cols = HEADS * HD
    slopes = jnp.exp2(-4.0 * jnp.arange(1, HEADS + 1, dtype=jnp.float32) / HEADS)
    qkv_matrix = w_qkv.reshape(D, 3 * head_cols)
    positions = jnp.arange(LMAX, dtype=jnp.int32)
    tok_ids = jnp.arange(TOK_DEV, dtype=jnp.int32)

    def one_shard(inputs):
        shard_tokens, shard_lengths, shard_slots = inputs
        starts = (jnp.cumsum(shard_lengths) - shard_lengths).astype(jnp.int32)
        live_rows = positions[None, :] < shard_lengths[:, None]
        row_index = jnp.minimum(starts[:, None] + positions[None, :], TOK_DEV - 1).astype(jnp.int32)
        gathered = jnp.where(live_rows[..., None], shard_tokens[row_index], jnp.zeros((), jnp.bfloat16))
        normed = layer_norm(gathered.reshape(R_DEV * LMAX, D), ln_gain, ln_bias)
        projected = jnp.dot(normed, qkv_matrix, preferred_element_type=jnp.float32) + qkv_bias.reshape(-1).astype(jnp.float32)
        projected = projected.reshape(R_DEV, LMAX, 3, HEADS, HD)
        live_mask = live_rows[:, :, None, None]
        queries = projected[:, :, 0].astype(jnp.bfloat16)
        new_keys = jnp.where(live_mask, projected[:, :, 1], 0.0).astype(jnp.bfloat16)
        new_vals = jnp.where(live_mask, projected[:, :, 2], 0.0).astype(jnp.bfloat16)
        stored = prefix_kv[shard_slots].reshape(R_DEV, PRE, 2, HEADS, HD)
        all_keys = jnp.concatenate([stored[:, :, 0], new_keys], axis=1)
        all_values = jnp.concatenate([stored[:, :, 1], new_vals], axis=1)
        context = attend(queries, all_keys, all_values, slopes, PRE)
        flat_context = context.reshape(R_DEV * LMAX, N_TP, head_cols // N_TP).astype(jnp.float32)
        head_terms = jnp.einsum('tni,nid->tnd', flat_context, w_dense.reshape(N_TP, head_cols // N_TP, D).astype(jnp.float32))
        rounded = lax.optimization_barrier(head_terms.astype(jnp.bfloat16))
        summed = lax.optimization_barrier(jnp.sum(rounded.astype(jnp.float32), axis=1))
        out_slots = (summed + dense_bias.astype(jnp.float32)).astype(jnp.bfloat16).reshape(R_DEV, LMAX, D)
        token_req = (lax.optimization_barrier(jnp.sum((tok_ids[:, None] >= starts[None, :]).astype(jnp.int32), axis=1)) - 1).astype(jnp.int32)
        within = (tok_ids - starts[token_req]).astype(jnp.int32)
        out_tokens = out_slots[token_req, within]
        fresh = jnp.stack([new_keys.reshape(R_DEV, LMAX, head_cols), new_vals.reshape(R_DEV, LMAX, head_cols)], axis=2)
        return (out_tokens, fresh)
    outs, fresh = lax.map(one_shard, (tokens.reshape(SHARDS, TOK_DEV, D), lengths, owner_slot.reshape(SHARDS, R_DEV)))
    new_cache = jnp.zeros((REQS, LMAX, 2, head_cols), jnp.bfloat16).at[owner_slot].set(fresh.reshape(REQS, LMAX, 2, head_cols))
    return (outs.reshape(TOKENS, D), new_cache)
```

```python
import functools
import math

import jax
import jax.numpy as jnp
from jax import lax
from jax.experimental import pallas as pl
from jax.experimental.pallas import tpu as pltpu
from jax.sharding import PartitionSpec as P

D = 2048
HD = 128
HEADS = 8
LMAX = 16
PRE = 32
BF = jnp.bfloat16
F32 = jnp.float32
VM = pl.BlockSpec(memory_space=pltpu.VMEM)
SM = pl.BlockSpec(memory_space=pltpu.SMEM)
ANY = pl.BlockSpec(memory_space=pl.ANY)


def iota(shape, dim):
    return lax.broadcasted_iota(jnp.int32, shape, dim)


def place_kernel(where_ref, src_ref, out_ref, sems):
    count = src_ref.shape[0]
    copies = [
        pltpu.make_async_copy(src_ref.at[j], out_ref.at[where_ref[j]], sems.at[j]) for j in range(count)
    ]
    for copy in copies:
        copy.start()
    for copy in copies:
        copy.wait()


def place(blocks, where, count):
    return pl.pallas_call(
        place_kernel,
        out_shape=jax.ShapeDtypeStruct((count,) + blocks.shape[1:], blocks.dtype),
        in_specs=[SM, ANY],
        out_specs=ANY,
        scratch_shapes=[pltpu.SemaphoreType.DMA((blocks.shape[0],))],
        name="place",
    )(where, blocks)


def fetch_kernel(where_ref, src_ref, out_ref, sems):
    count = out_ref.shape[0]
    copies = [
        pltpu.make_async_copy(src_ref.at[where_ref[j]], out_ref.at[j], sems.at[j]) for j in range(count)
    ]
    for copy in copies:
        copy.start()
    for copy in copies:
        copy.wait()


def fetch(blocks, where):
    count = where.shape[0]
    return pl.pallas_call(
        fetch_kernel,
        out_shape=jax.ShapeDtypeStruct((count,) + blocks.shape[1:], blocks.dtype),
        in_specs=[SM, ANY],
        out_specs=ANY,
        scratch_shapes=[pltpu.SemaphoreType.DMA((count,))],
        name="fetch",
    )(where, blocks)


def project_kernel(
    starts_ref, sizes_ref, dest_ref, rows_ref, w_ref, bias_ref, q_ref, new_ref, send_ref, sems
):
    tok = rows_ref.shape[0] - 8
    reqs = new_ref.shape[0]
    values = rows_ref[pl.ds(0, tok), :].astype(F32)
    width = values.shape[1]
    mean_val = jnp.sum(values, axis=1, keepdims=True) / width
    second = jnp.sum(values * values, axis=1, keepdims=True) / width
    scale_inv = lax.rsqrt(second - mean_val * mean_val + 1e-05)
    tail = rows_ref[pl.ds(tok, 8), :].astype(F32)
    normed = ((values - mean_val) * scale_inv * tail[0:1] + tail[1:2]).astype(BF)
    parts = [
        (
            jnp.dot(normed, w_ref[i], preferred_element_type=F32)
            + bias_ref[pl.ds(i, 1), :].astype(F32)
        ).astype(BF)
        for i in range(3)
    ]
    place_of = iota((LMAX, tok), 1)
    turn = iota((LMAX, tok), 0)
    pair_place = iota((2 * LMAX, tok), 1)
    pair_turn = iota((2 * LMAX, tok), 0)
    half = pair_turn // 2
    is_key = (pair_turn % 2) == 0
    copies = []
    for j in range(reqs):
        start, size = starts_ref[j], sizes_ref[j]
        one = ((place_of - start) == turn) & (turn < size)
        q_ref[pl.ds(j * LMAX, LMAX), :] = jnp.dot(
            one.astype(F32).astype(BF), parts[0], preferred_element_type=F32
        ).astype(BF)
        hit = ((pair_place - start) == half) & (half < size)
        keys = (hit & is_key).astype(F32).astype(BF)
        vals = (hit & jnp.logical_not(is_key)).astype(F32).astype(BF)
        both = jnp.dot(keys, parts[1], preferred_element_type=F32) + jnp.dot(
            vals, parts[2], preferred_element_type=F32
        )
        new_ref[j] = both.astype(BF)
        copy = pltpu.make_async_copy(new_ref.at[j], send_ref.at[dest_ref[j]], sems.at[j])
        copy.start()
        copies.append(copy)
    for copy in copies:
        copy.wait()


def project(starts, sizes, dest, rows, w, bias, shards):
    reqs = starts.shape[0]
    return pl.pallas_call(
        project_kernel,
        out_shape=(
            jax.ShapeDtypeStruct((reqs * LMAX, HD), BF),
            jax.ShapeDtypeStruct((reqs, 2 * LMAX, HD), BF),
            jax.ShapeDtypeStruct((shards, 2 * LMAX, HD), BF),
        ),
        in_specs=[SM, SM, SM, VM, VM, VM],
        out_specs=(VM, VM, ANY),
        scratch_shapes=[pltpu.SemaphoreType.DMA((reqs,))],
        name="project",
    )(starts, sizes, dest, rows, w, bias)


def attend_kernel(
    starts_ref, sizes_ref, dest_ref, slope_ref, q_ref, new_ref, came_ref, out_ref, kv, logits, mixed, sems
):
    reqs = new_ref.shape[0]
    tok = out_ref.shape[0]
    span = 2 * (PRE + LMAX)
    copies = []
    for j in range(reqs):
        copy = pltpu.make_async_copy(came_ref.at[dest_ref[j]], kv.at[j, pl.ds(0, 2 * PRE)], sems.at[j])
        copy.start()
        copies.append(copy)
    for j in range(reqs):
        kv[j, pl.ds(2 * PRE, 2 * LMAX), :] = new_ref[j]
        kv[j, pl.ds(span, 128 - span), :] = jnp.zeros((128 - span, HD), BF)
    for j in range(reqs):
        copies[j].wait()
    for j in range(reqs):
        logits[pl.ds(j * LMAX, LMAX), :] = lax.dot_general(
            q_ref[pl.ds(j * LMAX, LMAX), :],
            kv[j],
            (((1,), (1,)), ((), ())),
            preferred_element_type=F32,
        )
    shape = (reqs * LMAX, 128)
    col = iota(shape, 1)
    turn = iota(shape, 0) % LMAX
    distance = PRE + turn - col // 2
    valid = (col % 2 == 0) & (col < span) & (distance >= 0)
    scores = logits[...] / math.sqrt(HD) - slope_ref[0] * distance.astype(F32)
    scores = jnp.where(valid, scores, -1e30)
    row_max = jnp.max(scores, axis=-1, keepdims=True)
    raised = jnp.where(valid, jnp.exp(scores - row_max), 0.0)
    weights = raised / jnp.sum(raised, axis=-1, keepdims=True)
    weights = pltpu.roll(weights, 1, 1).astype(BF)
    for j in range(reqs):
        mixed[pl.ds(j * LMAX, LMAX), :] = jnp.dot(
            weights[j * LMAX : (j + 1) * LMAX], kv[j], preferred_element_type=F32
        ).astype(BF)
    lane = iota((1, reqs * LMAX), 1)
    row_of = jnp.full((1, reqs * LMAX), -1, jnp.int32)
    for j in range(reqs):
        step = lane - j * LMAX
        row_of = jnp.where((step >= 0) & (step < sizes_ref[j]), starts_ref[j] + step, row_of)
    pick = (iota((tok, reqs * LMAX), 0) == row_of).astype(F32).astype(BF)
    out_ref[...] = jnp.dot(pick, mixed[...], preferred_element_type=F32).astype(BF)


def attend(starts, sizes, dest, slope, q, new, came, tok):
    reqs = starts.shape[0]
    return pl.pallas_call(
        attend_kernel,
        out_shape=jax.ShapeDtypeStruct((tok, HD), BF),
        in_specs=[SM, SM, SM, SM, VM, VM, ANY],
        out_specs=VM,
        scratch_shapes=[
            pltpu.VMEM((reqs, 128, HD), BF),
            pltpu.VMEM((reqs * LMAX, 128), F32),
            pltpu.VMEM((reqs * LMAX, HD), BF),
            pltpu.SemaphoreType.DMA((reqs,)),
        ],
        name="attend",
    )(starts, sizes, dest, slope, q, new, came)


def dense_kernel(rank_ref, ctx_ref, own_ref, other_ref, mine_ref, *out_refs):
    rank = rank_ref[0]
    side = lax.rem(rank, 2)
    place_at = rank // 2
    tok = mine_ref.shape[0]
    cols = mine_ref.shape[1]
    own_ctx = ctx_ref[side]
    other_ctx = ctx_ref[1 - side]
    count = len(out_refs) + 1
    for s in range(count):
        block = lax.rem(place_at + s, count)
        total = jnp.dot(
            own_ctx, own_ref[:, pl.ds(pl.multiple_of((2 * block + side) * cols, cols), cols)],
            preferred_element_type=F32,
        ) + jnp.dot(
            other_ctx, other_ref[:, pl.ds(pl.multiple_of(block * cols, cols), cols)],
            preferred_element_type=F32,
        )
        if s == 0:
            mine_ref[...] = total
        else:
            out_refs[s - 1][...] = total.astype(BF)


def dense(rank, ctx, own, other, cols):
    tok = ctx.shape[1]
    count = other.shape[1] // cols
    return pl.pallas_call(
        dense_kernel,
        out_shape=[jax.ShapeDtypeStruct((tok, cols), F32)]
        + [jax.ShapeDtypeStruct((tok, cols), BF)] * (count - 1),
        in_specs=[SM, VM, VM, VM],
        out_specs=[VM] * count,
        name="dense",
    )(rank, ctx, own, other)


def per_device(
    tokens, ln_gain, ln_bias, w_qkv, qkv_bias, w_dense, dense_bias, prefix_kv, lengths, owner_slot
):
    shards = lax.axis_size("req")
    ranks = lax.axis_size("tp")
    req_rank = lax.axis_index("req")
    tp_rank = lax.axis_index("tp")
    tok_dev, part_cols = tokens.shape
    reqs_dev = lengths.shape[1]
    owners = (owner_slot // reqs_dev).reshape(shards, reqs_dev)
    shard_ids = jnp.arange(shards, dtype=jnp.int32)[:, None]
    source_of = jnp.sum(jnp.where(owners == req_rank, shard_ids, 0), axis=0)
    own_sizes = jnp.sum(jnp.where(shard_ids == req_rank, lengths, 0), axis=0)
    own_dest = jnp.sum(jnp.where(shard_ids == req_rank, owners, 0), axis=0)
    slot_ids = jnp.arange(reqs_dev, dtype=jnp.int32)
    own_starts = jnp.sum(
        jnp.where(slot_ids[:, None] < slot_ids[None, :], own_sizes[:, None], 0), axis=0
    )

    prefix_out = place(prefix_kv.reshape(reqs_dev, 2 * PRE, HD), source_of, shards)
    prefix_in = lax.all_to_all(prefix_out, "req", split_axis=0, concat_axis=0, tiled=True)

    side = lax.rem(tp_rank, 2)
    split = w_dense.reshape(HD, ranks // 2, 2, part_cols)
    give = jnp.where(side == 0, split[:, :, 1], split[:, :, 0]).reshape(HD, -1)
    other_w = lax.ppermute(give, "tp", [(i, i ^ 1) for i in range(ranks)])

    rows = jnp.concatenate(
        [tokens, ln_gain[None], ln_bias[None], jnp.zeros((6, part_cols), tokens.dtype)], axis=0
    )
    rows = lax.all_gather(rows, "tp", axis=1, tiled=True)
    queries, fresh, fresh_out = project(
        own_starts, own_sizes, own_dest, rows, jnp.transpose(w_qkv, (1, 0, 2)), qkv_bias, shards
    )
    fresh_in = lax.all_to_all(fresh_out, "req", split_axis=0, concat_axis=0, tiled=True)

    slope = jnp.exp2(-4.0 * (tp_rank + 1).astype(F32) / HEADS).reshape(1)
    context = attend(own_starts, own_sizes, own_dest, slope, queries, fresh, prefix_in, tok_dev)
    pairs = [[i, i + 1] for i in range(0, ranks, 2)]
    both = lax.all_gather(context, "tp", axis=0, tiled=False, axis_index_groups=pairs)
    mine, *others = dense(tp_rank.reshape(1), both, w_dense, other_w, part_cols)
    total = mine
    for s, other in enumerate(others):
        total = total + lax.ppermute(
            other, "tp", [(i, (i + 2 * (s + 1)) % ranks) for i in range(ranks)]
        ).astype(F32)
    output = (total + dense_bias.astype(F32)).astype(BF)
    new_cache = fetch(fresh_in, source_of).reshape(reqs_dev, LMAX, 2, HD)
    return (output, new_cache)


def solution(mesh):
    return jax.shard_map(
        per_device,
        mesh=mesh,
        in_specs=(
            P("req", "tp"),
            P("tp"),
            P("tp"),
            P(None, None, "tp"),
            P(None, "tp"),
            P("tp", None),
            P("tp"),
            P("req", None, None, "tp"),
            P(),
            P(),
        ),
        out_specs=(P("req", "tp"), P("req", None, None, "tp")),
        check_vma=False,
    )
```

```python
import functools
import math

import jax
import jax.numpy as jnp
from jax import lax
from jax.experimental import pallas as pl
from jax.experimental.pallas import tpu as pltpu
from jax.sharding import PartitionSpec as P

D = 2048
HD = 128
HEADS = 8
LMAX = 16
PRE = 32
BF = jnp.bfloat16
F32 = jnp.float32
VM = pl.BlockSpec(memory_space=pltpu.VMEM)
SM = pl.BlockSpec(memory_space=pltpu.SMEM)
ANY = pl.BlockSpec(memory_space=pl.ANY)


def iota(shape, dim):
    return lax.broadcasted_iota(jnp.int32, shape, dim)


def place_kernel(source_ref, tp_ref, src_ref, own_ref, out_ref, give_ref, sems):
    copies = [
        pltpu.make_async_copy(src_ref.at[j], out_ref.at[source_ref[j]], sems.at[j])
        for j in range(src_ref.shape[0])
    ]
    for copy in copies:
        copy.start()
    cols = own_ref.shape[1] // HEADS
    other = 1 - lax.rem(tp_ref[0], 2)
    for b in range(HEADS // 2):
        give_ref[:, pl.ds(b * cols, cols)] = own_ref[
            :, pl.ds(pl.multiple_of((2 * b + other) * cols, cols), cols)
        ]
    for copy in copies:
        copy.wait()


def place(source, tp, blocks, own, count):
    return pl.pallas_call(
        place_kernel,
        out_shape=(
            jax.ShapeDtypeStruct((count,) + blocks.shape[1:], blocks.dtype),
            jax.ShapeDtypeStruct((own.shape[0], own.shape[1] // 2), own.dtype),
        ),
        in_specs=[SM, SM, VM, VM],
        out_specs=(ANY, VM),
        scratch_shapes=[pltpu.SemaphoreType.DMA((blocks.shape[0],))],
        name="place",
    )(source, tp, blocks, own)


def fetch_kernel(where_ref, src_ref, out_ref, sems):
    count = out_ref.shape[0]
    copies = [
        pltpu.make_async_copy(src_ref.at[where_ref[j]], out_ref.at[j], sems.at[j]) for j in range(count)
    ]
    for copy in copies:
        copy.start()
    for copy in copies:
        copy.wait()


def fetch(blocks, where):
    count = where.shape[0]
    return pl.pallas_call(
        fetch_kernel,
        out_shape=jax.ShapeDtypeStruct((count,) + blocks.shape[1:], blocks.dtype),
        in_specs=[SM, ANY],
        out_specs=VM,
        scratch_shapes=[pltpu.SemaphoreType.DMA((count,))],
        name="fetch",
    )(where, blocks)


def requests(rank_ref, lengths_ref, owner_ref):
    count = lengths_ref.shape[0]
    rank = rank_ref[0]
    found, start = [], jnp.int32(0)
    for j in range(count):
        size = lengths_ref[j, rank]
        found.append((start, size, owner_ref[rank * count + j] // count))
        start = start + size
    return found


def project_kernel(
    rank_ref, lengths_ref, owner_ref, rows_ref, w_ref, bias_ref, q_ref, new_ref, send_ref, sems
):
    tok = rows_ref.shape[0] - 8
    reqs = new_ref.shape[0]
    values = rows_ref[pl.ds(0, tok), :].astype(F32)
    width = values.shape[1]
    mean_val = jnp.sum(values, axis=1, keepdims=True) / width
    second = jnp.sum(values * values, axis=1, keepdims=True) / width
    scale_inv = lax.rsqrt(second - mean_val * mean_val + 1e-05)
    tail = rows_ref[pl.ds(tok, 8), :].astype(F32)
    normed = ((values - mean_val) * scale_inv * tail[0:1] + tail[1:2]).astype(BF)
    parts = [
        (
            jnp.dot(normed, w_ref[i], preferred_element_type=F32)
            + bias_ref[pl.ds(i, 1), :].astype(F32)
        ).astype(BF)
        for i in range(3)
    ]
    found = requests(rank_ref, lengths_ref, owner_ref)
    gap = iota((LMAX, tok), 1) - iota((LMAX, tok), 0)
    turn = iota((LMAX, tok), 0)
    one = [(gap == start) & (turn < size) for start, size, _ in found]
    one = jnp.concatenate([hit.astype(F32) for hit in one], axis=0).astype(BF)
    q_ref[...] = jnp.dot(one, parts[0], preferred_element_type=F32).astype(BF)
    half = iota((2 * LMAX, tok), 0) // 2
    gap = iota((2 * LMAX, tok), 1) - half
    even = (iota((2 * LMAX, tok), 0) % 2 == 0).astype(F32)
    hits = [((gap == start) & (half < size)).astype(F32) for start, size, _ in found]
    keys = jnp.concatenate([hit * even for hit in hits], axis=0).astype(BF)
    vals = jnp.concatenate([hit * (1.0 - even) for hit in hits], axis=0).astype(BF)
    both = jnp.dot(keys, parts[1], preferred_element_type=F32) + jnp.dot(
        vals, parts[2], preferred_element_type=F32
    )
    new_ref[...] = both.astype(BF).reshape(reqs, 2 * LMAX, HD)
    copies = [
        pltpu.make_async_copy(new_ref.at[j], send_ref.at[found[j][2]], sems.at[j]) for j in range(reqs)
    ]
    for copy in copies:
        copy.start()
    for copy in copies:
        copy.wait()


def project(rank, lengths, owner, rows, w, bias, shards):
    reqs = lengths.shape[0]
    return pl.pallas_call(
        project_kernel,
        out_shape=(
            jax.ShapeDtypeStruct((reqs * LMAX, HD), BF),
            jax.ShapeDtypeStruct((reqs, 2 * LMAX, HD), BF),
            jax.ShapeDtypeStruct((shards, 2 * LMAX, HD), BF),
        ),
        in_specs=[SM, SM, SM, VM, VM, VM],
        out_specs=(VM, VM, ANY),
        scratch_shapes=[pltpu.SemaphoreType.DMA((reqs,))],
        name="project",
    )(rank, lengths, owner, rows, w, bias)


def attend_kernel(
    rank_ref, lengths_ref, owner_ref, slope_ref, q_ref, new_ref, came_ref, out_ref, kv, logits, mixed, sems
):
    reqs = new_ref.shape[0]
    tok = out_ref.shape[0]
    span = 2 * (PRE + LMAX)
    found = requests(rank_ref, lengths_ref, owner_ref)
    copies = []
    for j in range(reqs):
        copy = pltpu.make_async_copy(came_ref.at[found[j][2]], kv.at[j, pl.ds(0, 2 * PRE)], sems.at[j])
        copy.start()
        copies.append(copy)
    for j in range(reqs):
        kv[j, pl.ds(2 * PRE, 2 * LMAX), :] = new_ref[j]
        kv[j, pl.ds(span, 128 - span), :] = jnp.zeros((128 - span, HD), BF)
    for j in range(reqs):
        copies[j].wait()
    for j in range(reqs):
        logits[pl.ds(j * LMAX, LMAX), :] = lax.dot_general(
            q_ref[pl.ds(j * LMAX, LMAX), :],
            kv[j],
            (((1,), (1,)), ((), ())),
            preferred_element_type=F32,
        )
    shape = (reqs * LMAX, 128)
    col = iota(shape, 1)
    turn = iota(shape, 0) % LMAX
    distance = PRE + turn - col // 2
    valid = (col % 2 == 0) & (col < span) & (distance >= 0)
    scores = logits[...] / math.sqrt(HD) - slope_ref[0] * distance.astype(F32)
    scores = jnp.where(valid, scores, -1e30)
    row_max = jnp.max(scores, axis=-1, keepdims=True)
    raised = jnp.where(valid, jnp.exp(scores - row_max), 0.0)
    weights = raised / jnp.sum(raised, axis=-1, keepdims=True)
    weights = pltpu.roll(weights, 1, 1).astype(BF)
    for j in range(reqs):
        mixed[pl.ds(j * LMAX, LMAX), :] = jnp.dot(
            weights[j * LMAX : (j + 1) * LMAX], kv[j], preferred_element_type=F32
        ).astype(BF)
    lane = iota((1, reqs * LMAX), 1)
    row_of = jnp.full((1, reqs * LMAX), -1, jnp.int32)
    for j in range(reqs):
        step = lane - j * LMAX
        start, size, _ = found[j]
        row_of = jnp.where((step >= 0) & (step < size), start + step, row_of)
    pick = (iota((tok, reqs * LMAX), 0) == row_of).astype(F32).astype(BF)
    out_ref[...] = jnp.dot(pick, mixed[...], preferred_element_type=F32).astype(BF)


def attend(rank, lengths, owner, slope, q, new, came, tok):
    reqs = lengths.shape[0]
    return pl.pallas_call(
        attend_kernel,
        out_shape=jax.ShapeDtypeStruct((tok, HD), BF),
        in_specs=[SM, SM, SM, SM, VM, VM, ANY],
        out_specs=VM,
        scratch_shapes=[
            pltpu.VMEM((reqs, 128, HD), BF),
            pltpu.VMEM((reqs * LMAX, 128), F32),
            pltpu.VMEM((reqs * LMAX, HD), BF),
            pltpu.SemaphoreType.DMA((reqs,)),
        ],
        name="attend",
    )(rank, lengths, owner, slope, q, new, came)


def dense_kernel(rank_ref, ctx_ref, own_ref, other_ref, mine_ref, *out_refs):
    rank = rank_ref[0]
    side = lax.rem(rank, 2)
    place_at = rank // 2
    tok = mine_ref.shape[0]
    cols = mine_ref.shape[1]
    own_ctx = ctx_ref[side]
    other_ctx = ctx_ref[1 - side]
    count = len(out_refs) + 1
    for s in range(count):
        block = lax.rem(place_at + s, count)
        total = jnp.dot(
            own_ctx, own_ref[:, pl.ds(pl.multiple_of((2 * block + side) * cols, cols), cols)],
            preferred_element_type=F32,
        ) + jnp.dot(
            other_ctx, other_ref[:, pl.ds(pl.multiple_of(block * cols, cols), cols)],
            preferred_element_type=F32,
        )
        if s == 0:
            mine_ref[...] = total
        else:
            out_refs[s - 1][...] = total.astype(BF)


def dense(rank, ctx, own, other, cols):
    tok = ctx.shape[1]
    count = other.shape[1] // cols
    return pl.pallas_call(
        dense_kernel,
        out_shape=[jax.ShapeDtypeStruct((tok, cols), F32)]
        + [jax.ShapeDtypeStruct((tok, cols), BF)] * (count - 1),
        in_specs=[SM, VM, VM, VM],
        out_specs=[VM] * count,
        name="dense",
    )(rank, ctx, own, other)


def per_device(
    tokens, ln_gain, ln_bias, w_qkv, qkv_bias, w_dense, dense_bias, prefix_kv, lengths, owner_slot
):
    shards = lax.axis_size("req")
    ranks = lax.axis_size("tp")
    req_rank = lax.axis_index("req")
    tp_rank = lax.axis_index("tp")
    tok_dev, part_cols = tokens.shape
    reqs_dev = lengths.shape[1]
    rank = req_rank.astype(jnp.int32).reshape(1)
    table = jnp.transpose(lengths)
    slots = req_rank * reqs_dev + jnp.arange(reqs_dev, dtype=jnp.int32)
    source_ids = jnp.arange(shards * reqs_dev, dtype=jnp.int32) // reqs_dev
    source_of = jnp.sum(jnp.where(owner_slot[None, :] == slots[:, None], source_ids[None, :], 0), axis=1)

    prefix_out, give = place(
        source_of, tp_rank.reshape(1), prefix_kv.reshape(reqs_dev, 2 * PRE, HD), w_dense, shards
    )
    prefix_in = lax.all_to_all(prefix_out, "req", split_axis=0, concat_axis=0, tiled=True)
    other_w = lax.ppermute(give, "tp", [(i, i ^ 1) for i in range(ranks)])

    rows = jnp.concatenate(
        [tokens, ln_gain[None], ln_bias[None], jnp.zeros((6, part_cols), tokens.dtype)], axis=0
    )
    rows = lax.all_gather(rows, "tp", axis=1, tiled=True)
    queries, fresh, fresh_out = project(
        rank, table, owner_slot, rows, jnp.transpose(w_qkv, (1, 0, 2)), qkv_bias, shards
    )
    fresh_in = lax.all_to_all(fresh_out, "req", split_axis=0, concat_axis=0, tiled=True)

    slope = jnp.exp2(-4.0 * (tp_rank + 1).astype(F32) / HEADS).reshape(1)
    context = attend(rank, table, owner_slot, slope, queries, fresh, prefix_in, tok_dev)
    pairs = [[i, i + 1] for i in range(0, ranks, 2)]
    both = lax.all_gather(context, "tp", axis=0, tiled=False, axis_index_groups=pairs)
    mine, *others = dense(tp_rank.reshape(1), both, w_dense, other_w, part_cols)
    total = mine
    for s, other in enumerate(others):
        total = total + lax.ppermute(
            other, "tp", [(i, (i + 2 * (s + 1)) % ranks) for i in range(ranks)]
        ).astype(F32)
    output = (total + dense_bias.astype(F32)).astype(BF)
    new_cache = fetch(fresh_in, source_of).reshape(reqs_dev, LMAX, 2, HD)
    return (output, new_cache)


def solution(mesh):
    return jax.shard_map(
        per_device,
        mesh=mesh,
        in_specs=(
            P("req", "tp"),
            P("tp"),
            P("tp"),
            P(None, None, "tp"),
            P(None, "tp"),
            P("tp", None),
            P("tp"),
            P("req", None, None, "tp"),
            P(),
            P(),
        ),
        out_specs=(P("req", "tp"), P("req", None, None, "tp")),
        check_vma=False,
    )
```

```python
import functools
import math

import jax
import jax.numpy as jnp
from jax import lax
from jax.experimental import pallas as pl
from jax.experimental.pallas import tpu as pltpu
from jax.sharding import PartitionSpec as P

D = 2048
HD = 128
HEADS = 8
LMAX = 16
PRE = 32
BF = jnp.bfloat16
F32 = jnp.float32
VM = pl.BlockSpec(memory_space=pltpu.VMEM)
SM = pl.BlockSpec(memory_space=pltpu.SMEM)
ANY = pl.BlockSpec(memory_space=pl.ANY)


def iota(shape, dim):
    return lax.broadcasted_iota(jnp.int32, shape, dim)


def place_kernel(source_ref, tp_ref, src_ref, own_ref, out_ref, give_ref, sems):
    copies = [
        pltpu.make_async_copy(src_ref.at[j], out_ref.at[source_ref[j]], sems.at[j])
        for j in range(src_ref.shape[0])
    ]
    for copy in copies:
        copy.start()
    cols = own_ref.shape[1] // HEADS
    rank = tp_ref[0]
    way = 2 * lax.rem(rank, 2) - 1
    for b in range(HEADS // 2):
        block = lax.rem(rank - way * (b + 1) + HEADS, HEADS)
        give_ref[:, pl.ds(b * cols, cols)] = own_ref[
            :, pl.ds(pl.multiple_of(block * cols, cols), cols)
        ]
    for copy in copies:
        copy.wait()


def place(source, tp, blocks, own, count):
    return pl.pallas_call(
        place_kernel,
        out_shape=(
            jax.ShapeDtypeStruct((count,) + blocks.shape[1:], blocks.dtype),
            jax.ShapeDtypeStruct((own.shape[0], own.shape[1] // 2), own.dtype),
        ),
        in_specs=[SM, SM, VM, VM],
        out_specs=(ANY, VM),
        scratch_shapes=[pltpu.SemaphoreType.DMA((blocks.shape[0],))],
        name="place",
    )(source, tp, blocks, own)


def fetch_kernel(where_ref, src_ref, out_ref, sems):
    count = out_ref.shape[0]
    copies = [
        pltpu.make_async_copy(src_ref.at[where_ref[j]], out_ref.at[j], sems.at[j]) for j in range(count)
    ]
    for copy in copies:
        copy.start()
    for copy in copies:
        copy.wait()


def fetch(blocks, where):
    count = where.shape[0]
    return pl.pallas_call(
        fetch_kernel,
        out_shape=jax.ShapeDtypeStruct((count,) + blocks.shape[1:], blocks.dtype),
        in_specs=[SM, ANY],
        out_specs=VM,
        scratch_shapes=[pltpu.SemaphoreType.DMA((count,))],
        name="fetch",
    )(where, blocks)


def requests(rank_ref, lengths_ref, owner_ref):
    count = lengths_ref.shape[0]
    rank = rank_ref[0]
    found, start = [], jnp.int32(0)
    for j in range(count):
        size = lengths_ref[j, rank]
        found.append((start, size, owner_ref[rank * count + j] // count))
        start = start + size
    return found


def project_kernel(
    rank_ref, lengths_ref, owner_ref, rows_ref, w_ref, bias_ref, q_ref, new_ref, send_ref, sems
):
    tok = rows_ref.shape[0] - 8
    reqs = new_ref.shape[0]
    values = rows_ref[pl.ds(0, tok), :].astype(F32)
    width = values.shape[1]
    mean_val = jnp.sum(values, axis=1, keepdims=True) / width
    second = jnp.sum(values * values, axis=1, keepdims=True) / width
    scale_inv = lax.rsqrt(second - mean_val * mean_val + 1e-05)
    tail = rows_ref[pl.ds(tok, 8), :].astype(F32)
    normed = ((values - mean_val) * scale_inv * tail[0:1] + tail[1:2]).astype(BF)
    parts = [
        (
            jnp.dot(normed, w_ref[i], preferred_element_type=F32)
            + bias_ref[pl.ds(i, 1), :].astype(F32)
        ).astype(BF)
        for i in range(3)
    ]
    found = requests(rank_ref, lengths_ref, owner_ref)
    gap = iota((LMAX, tok), 1) - iota((LMAX, tok), 0)
    turn = iota((LMAX, tok), 0)
    one = [(gap == start) & (turn < size) for start, size, _ in found]
    one = jnp.concatenate([hit.astype(F32) for hit in one], axis=0).astype(BF)
    q_ref[...] = jnp.dot(one, parts[0], preferred_element_type=F32).astype(BF)
    half = iota((2 * LMAX, tok), 0) // 2
    gap = iota((2 * LMAX, tok), 1) - half
    even = (iota((2 * LMAX, tok), 0) % 2 == 0).astype(F32)
    hits = [((gap == start) & (half < size)).astype(F32) for start, size, _ in found]
    keys = jnp.concatenate([hit * even for hit in hits], axis=0).astype(BF)
    vals = jnp.concatenate([hit * (1.0 - even) for hit in hits], axis=0).astype(BF)
    both = jnp.dot(keys, parts[1], preferred_element_type=F32) + jnp.dot(
        vals, parts[2], preferred_element_type=F32
    )
    new_ref[...] = both.astype(BF).reshape(reqs, 2 * LMAX, HD)
    copies = [
        pltpu.make_async_copy(new_ref.at[j], send_ref.at[found[j][2]], sems.at[j]) for j in range(reqs)
    ]
    for copy in copies:
        copy.start()
    for copy in copies:
        copy.wait()


def project(rank, lengths, owner, rows, w, bias, shards):
    reqs = lengths.shape[0]
    return pl.pallas_call(
        project_kernel,
        out_shape=(
            jax.ShapeDtypeStruct((reqs * LMAX, HD), BF),
            jax.ShapeDtypeStruct((reqs, 2 * LMAX, HD), BF),
            jax.ShapeDtypeStruct((shards, 2 * LMAX, HD), BF),
        ),
        in_specs=[SM, SM, SM, VM, VM, VM],
        out_specs=(VM, VM, ANY),
        scratch_shapes=[pltpu.SemaphoreType.DMA((reqs,))],
        name="project",
    )(rank, lengths, owner, rows, w, bias)


def attend_kernel(
    rank_ref, lengths_ref, owner_ref, slope_ref, q_ref, new_ref, came_ref, out_ref, kv, logits, mixed, sems
):
    reqs = new_ref.shape[0]
    tok = out_ref.shape[0]
    span = 2 * (PRE + LMAX)
    found = requests(rank_ref, lengths_ref, owner_ref)
    copies = []
    for j in range(reqs):
        copy = pltpu.make_async_copy(came_ref.at[found[j][2]], kv.at[j, pl.ds(0, 2 * PRE)], sems.at[j])
        copy.start()
        copies.append(copy)
    for j in range(reqs):
        kv[j, pl.ds(2 * PRE, 2 * LMAX), :] = new_ref[j]
        kv[j, pl.ds(span, 128 - span), :] = jnp.zeros((128 - span, HD), BF)
    for j in range(reqs):
        copies[j].wait()
    for j in range(reqs):
        logits[pl.ds(j * LMAX, LMAX), :] = lax.dot_general(
            q_ref[pl.ds(j * LMAX, LMAX), :],
            kv[j],
            (((1,), (1,)), ((), ())),
            preferred_element_type=F32,
        )
    shape = (reqs * LMAX, 128)
    col = iota(shape, 1)
    turn = iota(shape, 0) % LMAX
    distance = PRE + turn - col // 2
    valid = (col % 2 == 0) & (col < span) & (distance >= 0)
    scores = logits[...] / math.sqrt(HD) - slope_ref[0] * distance.astype(F32)
    scores = jnp.where(valid, scores, -1e30)
    row_max = jnp.max(scores, axis=-1, keepdims=True)
    raised = jnp.where(valid, jnp.exp(scores - row_max), 0.0)
    weights = raised / jnp.sum(raised, axis=-1, keepdims=True)
    weights = pltpu.roll(weights, 1, 1).astype(BF)
    for j in range(reqs):
        mixed[pl.ds(j * LMAX, LMAX), :] = jnp.dot(
            weights[j * LMAX : (j + 1) * LMAX], kv[j], preferred_element_type=F32
        ).astype(BF)
    lane = iota((1, reqs * LMAX), 1)
    row_of = jnp.full((1, reqs * LMAX), -1, jnp.int32)
    for j in range(reqs):
        step = lane - j * LMAX
        start, size, _ = found[j]
        row_of = jnp.where((step >= 0) & (step < size), start + step, row_of)
    pick = (iota((tok, reqs * LMAX), 0) == row_of).astype(F32).astype(BF)
    out_ref[...] = jnp.dot(pick, mixed[...], preferred_element_type=F32).astype(BF)


def attend(rank, lengths, owner, slope, q, new, came, tok):
    reqs = lengths.shape[0]
    return pl.pallas_call(
        attend_kernel,
        out_shape=jax.ShapeDtypeStruct((tok, HD), BF),
        in_specs=[SM, SM, SM, SM, VM, VM, ANY],
        out_specs=VM,
        scratch_shapes=[
            pltpu.VMEM((reqs, 128, HD), BF),
            pltpu.VMEM((reqs * LMAX, 128), F32),
            pltpu.VMEM((reqs * LMAX, HD), BF),
            pltpu.SemaphoreType.DMA((reqs,)),
        ],
        name="attend",
    )(rank, lengths, owner, slope, q, new, came)


def dense_kernel(rank_ref, ctx_ref, own_ref, other_ref, mine_ref, *out_refs):
    rank = rank_ref[0]
    side = lax.rem(rank, 2)
    way = 2 * side - 1
    cols = mine_ref.shape[1]
    own_ctx = ctx_ref[side]
    other_ctx = ctx_ref[1 - side]
    count = len(out_refs) + 1
    for s in range(count):
        block = lax.rem(rank + way * s + 2 * count, 2 * count)
        total = jnp.dot(
            own_ctx, own_ref[:, pl.ds(pl.multiple_of(block * cols, cols), cols)],
            preferred_element_type=F32,
        ) + jnp.dot(
            other_ctx, other_ref[:, pl.ds(s * cols, cols)],
            preferred_element_type=F32,
        )
        if s == 0:
            mine_ref[...] = total
        else:
            out_refs[s - 1][...] = total.astype(BF)


def dense(rank, ctx, own, other, cols):
    tok = ctx.shape[1]
    count = other.shape[1] // cols
    return pl.pallas_call(
        dense_kernel,
        out_shape=[jax.ShapeDtypeStruct((tok, cols), F32)]
        + [jax.ShapeDtypeStruct((tok, cols), BF)] * (count - 1),
        in_specs=[SM, VM, VM, VM],
        out_specs=[VM] * count,
        name="dense",
    )(rank, ctx, own, other)


def per_device(
    tokens, ln_gain, ln_bias, w_qkv, qkv_bias, w_dense, dense_bias, prefix_kv, lengths, owner_slot
):
    shards = lax.axis_size("req")
    ranks = lax.axis_size("tp")
    req_rank = lax.axis_index("req")
    tp_rank = lax.axis_index("tp")
    tok_dev, part_cols = tokens.shape
    reqs_dev = lengths.shape[1]
    rank = req_rank.astype(jnp.int32).reshape(1)
    table = jnp.transpose(lengths)
    slots = req_rank * reqs_dev + jnp.arange(reqs_dev, dtype=jnp.int32)
    source_ids = jnp.arange(shards * reqs_dev, dtype=jnp.int32) // reqs_dev
    source_of = jnp.sum(jnp.where(owner_slot[None, :] == slots[:, None], source_ids[None, :], 0), axis=1)

    prefix_out, give = place(
        source_of, tp_rank.reshape(1), prefix_kv.reshape(reqs_dev, 2 * PRE, HD), w_dense, shards
    )
    prefix_in = lax.all_to_all(prefix_out, "req", split_axis=0, concat_axis=0, tiled=True)
    other_w = lax.ppermute(give, "tp", [(i, i ^ 1) for i in range(ranks)])

    rows = jnp.concatenate(
        [tokens, ln_gain[None], ln_bias[None], jnp.zeros((6, part_cols), tokens.dtype)], axis=0
    )
    rows = lax.all_gather(rows, "tp", axis=1, tiled=True)
    queries, fresh, fresh_out = project(
        rank, table, owner_slot, rows, jnp.transpose(w_qkv, (1, 0, 2)), qkv_bias, shards
    )
    fresh_in = lax.all_to_all(fresh_out, "req", split_axis=0, concat_axis=0, tiled=True)

    slope = jnp.exp2(-4.0 * (tp_rank + 1).astype(F32) / HEADS).reshape(1)
    context = attend(rank, table, owner_slot, slope, queries, fresh, prefix_in, tok_dev)
    pairs = [[i, i + 1] for i in range(0, ranks, 2)]
    both = lax.all_gather(context, "tp", axis=0, tiled=False, axis_index_groups=pairs)
    mine, *others = dense(tp_rank.reshape(1), both, w_dense, other_w, part_cols)
    total = mine
    for s in range(len(others), 0, -1):
        route = [(i, (i + (s if i % 2 else -s)) % ranks) for i in range(ranks)]
        total = total + lax.ppermute(others[s - 1], "tp", route).astype(F32)
    output = (total + dense_bias.astype(F32)).astype(BF)
    new_cache = fetch(fresh_in, source_of).reshape(reqs_dev, LMAX, 2, HD)
    return (output, new_cache)


def solution(mesh):
    return jax.shard_map(
        per_device,
        mesh=mesh,
        in_specs=(
            P("req", "tp"),
            P("tp"),
            P("tp"),
            P(None, None, "tp"),
            P(None, "tp"),
            P("tp", None),
            P("tp"),
            P("req", None, None, "tp"),
            P(),
            P(),
        ),
        out_specs=(P("req", "tp"), P("req", None, None, "tp")),
        check_vma=False,
    )
```
